1024 devices in a mesh: batch: 16 (over z, core), proto: 64 (over y, x).
Axes of the slice: x: 8, y: 8, z: 8, core: 2. Of those that a mesh axis runs over, the one named last changes fastest.
Arguments:
- teacher: bfloat16 [64, 256, 256], P('batch'), may hold values from -1 to 1
- student: bfloat16 [64, 256, 256], P('batch'), may hold values from -0.5 to 0.5
- perm: int32 [64, 256], P('batch'), may hold values from 0 to 255, each once within a row
- counts: int32 [16, 4], P('batch'), may hold values from 1 to 128, 384 in all within a row
- prototypes: bfloat16 [256, 131072], P(None, 'proto'), may hold values from -1 to 1
Outputs:
- feature_grad: float32 [6144, 256], P(('batch', 'proto'))
- proto_grad: float32 [256, 131072], P('batch', 'proto')
The draws below stay inside these ranges and needn't reach their ends.
Inputs may be any that keep to these rules, and one draw needn't show every extreme that they name: Each row of counts sums to exactly 384; some image of each batch index has exactly 128 masked patches. Each row of perm is a permutation of the 256 patches; the first counts entries of an image's row are its masked patches.
All inputs are finite; a program needn't handle non-finite values.
Results may differ from the reference program's by a relative error of at most 0.0053.
Values sent between devices are 32-bit elements; how exact they have to be, the bound alone decides.
No kernel may reach another device: no remote copies, remote signals or barrier semaphores. Data moves between devices by JAX's collectives and lax.ppermute only.
A program may use at most 32 MiB of HBM per device.

```python
import math
import jax
import jax.numpy as jnp
import numpy as np
from jax import lax

BOT = 256
K = 131072
P_SIZE = 256
SWEEPS = 3
GROUP_ROWS = 384
IMG_GROUP = 4
IMAGES = 64
ROWS = 6144
N_BATCH = 16


cluster_total = 8


def cluster_signs(key):
    bits = jax.random.randint(jax.random.fold_in(key, 101), (cluster_total, BOT), 0, 2)
    return (bits.astype(jnp.float32) * 2.0 - 1.0) / jnp.sqrt(jnp.float32(BOT))


def draw_teacher(key, part):
    signs = cluster_signs(key)
    first = jax.random.randint(jax.random.fold_in(key, 102), (IMAGES,), 0, cluster_total)
    second = jax.random.randint(jax.random.fold_in(key, 103), (IMAGES,), 0, cluster_total)
    cluster = jnp.minimum(first, second)
    spread = 1.0 / jnp.sqrt(jnp.float32(BOT))
    noise = jax.random.normal(jax.random.fold_in(key, 104), (IMAGES, P_SIZE, BOT), jnp.float32) * spread
    lift = 0.225
    values = lift * signs[cluster][:, None, :] + noise
    return jnp.clip(values, -1.0, 1.0).astype(jnp.bfloat16)


def draw_prototypes(key, part):
    signs = cluster_signs(key)
    column_cluster = jnp.arange(K, dtype=jnp.int32) % cluster_total
    spread = 1.0 / jnp.sqrt(jnp.float32(BOT))
    noise = jax.random.normal(jax.random.fold_in(key, 105), (BOT, K), jnp.float32) * spread
    values = 0.5 * jnp.transpose(signs[column_cluster]) + noise
    return jnp.clip(values, -1.0, 1.0).astype(jnp.bfloat16)


def shard_levels(stream_key, extent, split, least, largest):
    level, own = 1.0, jax.random.fold_in(stream_key, 6)
    for dim, parts in split:
        draws = jnp.exp(jax.random.uniform(jax.random.fold_in(own, dim), (parts,), jnp.float32, least / len(split), largest / len(split)))
        level = level * jnp.repeat(draws, extent[dim] // parts).reshape([-1 if axis == dim else 1 for axis in range(len(extent))])
    return level


def length_profile(number_of, total, bound, lean):
    weights = [(1 << 20) // math.isqrt(grade ** lean) + 1 for grade in range(2, number_of + 1)]
    spare, holding = total - bound - (number_of - 1), [1] * (number_of - 1)
    while spare > 0:
        candidates = [i for i in range(number_of - 1) if holding[i] < bound]
        pool, left = sum([weights[i] for i in candidates]), spare
        for i in candidates:
            more = min(bound - holding[i], max(1, left * weights[i] // pool), spare)
            holding[i] = holding[i] + more
            spare = spare - more
    return np.array([bound] + holding)


def ragged(stream_key, number_of, total, limit, skew):
    if number_of == 2:
        one = jax.random.randint(stream_key, (), max(1, total - limit), min(limit, total - 1) + 1)
        return jnp.stack([one, total - one])
    lengths = jnp.asarray(length_profile(number_of, total, limit, skew), jnp.int32)
    couples = (number_of - 1) // 2
    donor, receiver = lengths[1:1 + 2 * couples:2], lengths[2:2 + 2 * couples:2]
    room = jnp.minimum(donor - 1, limit - receiver)
    moved = jax.random.randint(jax.random.fold_in(stream_key, 1), (couples,), 0, 1 << 20) % (room + 1)
    lengths = lengths.at[1:1 + 2 * couples:2].set(donor - moved).at[2:2 + 2 * couples:2].set(receiver + moved)
    return lengths[jax.random.permutation(jax.random.fold_in(stream_key, 2), number_of)]


def centred(stream_key, extent, width, reach, split=(), kind=jnp.bfloat16):
    array = jax.random.normal(stream_key, extent, jnp.float32) * width
    if len(split) > 0:
        array = shard_levels(stream_key, extent, split, -0.22, 0.18) * array
    return jnp.clip(array, min=-reach, max=reach).astype(kind)


def setup_inputs(seed: int = 0) -> dict:
    arg_keys = jax.random.split(jax.random.key(seed), 6)
    teacher = draw_teacher(jax.random.fold_in(arg_keys[5], 71), 0)
    student = centred(arg_keys[1], (IMAGES, P_SIZE, BOT), 0.0625, 0.5, ((0, 16),))
    perm = jax.vmap(lambda own: jax.random.permutation(own, P_SIZE))(jax.random.split(arg_keys[2], IMAGES)).reshape((IMAGES, P_SIZE)).astype(jnp.int32)
    counts = jax.vmap(lambda own: ragged(own, IMG_GROUP, GROUP_ROWS, P_SIZE // 2, 2))(jax.random.split(arg_keys[3], N_BATCH)).reshape((N_BATCH, IMG_GROUP)).astype(jnp.int32)
    prototypes = draw_prototypes(jax.random.fold_in(arg_keys[5], 71), 0)
    return {"teacher": teacher, "student": student, "perm": perm, "counts": counts, "prototypes": prototypes}


def layout(perm, counts):
    ends = jnp.cumsum(counts, axis=1)
    starts = ends - counts
    line = jnp.arange(GROUP_ROWS, dtype=jnp.int32)
    owner = lax.optimization_barrier(jnp.sum((ends[:, None, :] <= line[None, :, None]).astype(jnp.int32), axis=2))
    first = jnp.take_along_axis(starts, owner, axis=1)
    inner = (line[None, :] - first).astype(jnp.int32)
    image = (owner + (jnp.arange(N_BATCH, dtype=jnp.int32) * IMG_GROUP)[:, None]).astype(jnp.int32)
    patch = perm[image, inner]
    return (image.reshape(-1), patch.reshape(-1))

def unit_rows(rows):
    values = rows.astype(jnp.float32)
    inverse = lax.rsqrt(lax.optimization_barrier(jnp.sum(values * values, axis=1, keepdims=True)) + 1e-06)
    return (values * inverse, inverse)

def reference(teacher, student, perm, counts, prototypes):
    image, patch = layout(perm, counts)
    weight_row = 1.0 / counts.reshape(-1)[image].astype(jnp.float32)
    teach_unit, unused = unit_rows(teacher[image, patch])
    stud_unit, inverse = unit_rows(student[image, patch])
    teach_half = teach_unit.astype(jnp.bfloat16)
    stud_half = stud_unit.astype(jnp.bfloat16)
    energy = jnp.exp(jnp.dot(teach_half, prototypes, preferred_element_type=jnp.float32) * 25.0)
    row_scale = jnp.ones((ROWS,), jnp.float32)
    col_scale = jnp.ones((K,), jnp.float32)
    for sweep in range(SWEEPS):
        col_scale = 1.0 / jnp.dot(row_scale, energy, precision=lax.Precision.HIGHEST)
        row_scale = 1.0 / jnp.dot(energy, col_scale, precision=lax.Precision.HIGHEST)

    def group_step(total, item):
        half, block, scales, weights = item
        expo = jnp.exp(jnp.dot(half, prototypes, preferred_element_type=jnp.float32) * 10.0)
        soft = expo / lax.optimization_barrier(jnp.sum(expo, axis=1, keepdims=True))
        target = scales[:, None] * block * col_scale[None, :]
        grad = (K * 10.0 * weights[:, None] * (soft - target)).astype(jnp.bfloat16)
        total = total + lax.dot_general(half, grad, (((0,), (0,)), ((), ())), preferred_element_type=jnp.float32)
        back = lax.dot_general(grad, prototypes, (((1,), (1,)), ((), ())), preferred_element_type=jnp.float32)
        return (total, back)
    items = (stud_half.reshape(N_BATCH, GROUP_ROWS, BOT), energy.reshape(N_BATCH, GROUP_ROWS, K), row_scale.reshape(N_BATCH, GROUP_ROWS), weight_row.reshape(N_BATCH, GROUP_ROWS))
    proto_grad, back = lax.scan(group_step, jnp.zeros((BOT, K), jnp.float32), items)
    back = back.reshape(ROWS, BOT)
    feature_grad = inverse * (back - stud_unit * lax.optimization_barrier(jnp.sum(stud_unit * back, axis=1, keepdims=True)))
    return (feature_grad, proto_grad)
```

```python
import jax
import jax.numpy as jnp
from jax import lax
from jax.experimental import pallas as pl
from jax.experimental.pallas import tpu as pltpu
from jax.sharding import PartitionSpec as P

K = 131072
SWEEPS = 3
ROWS = 384
BOT = 256
COLS = 2048
PATCHES = 256
IMAGES = 4
HALF = COLS // 2
LANES = 128
NB = 16
NP = 64
NZ = 8
F32 = jnp.float32
BF16 = jnp.bfloat16


def unit_rows(values):
    inverse = lax.rsqrt(jnp.sum(values * values, axis=1, keepdims=True) + 1e-06)
    return values * inverse, inverse


def to_column(line):
    return jnp.broadcast_to(line, (LANES, ROWS)).T


def to_line(part):
    return jnp.sum(part.T, axis=0, keepdims=True)


def tile_sums(part):
    return jnp.concatenate([jnp.sum(p, axis=0, keepdims=True) for p in part], axis=0)


def start_body(counts, core, perm, teacher, student, protos, energy, col_out, rows_out, hs_out, keep_out, send_out, weight_out, ht):
    @pl.when(pl.program_id(0) == 0)
    def _():
        row = lax.broadcasted_iota(jnp.int32, (ROWS, PATCHES), 0)
        place = lax.broadcasted_iota(jnp.int32, (ROWS, PATCHES), 1)
        row_line = lax.broadcasted_iota(jnp.int32, (ROWS, LANES), 0)
        found = jnp.zeros((ROWS, PATCHES), F32)
        owned = jnp.zeros((ROWS, LANES), F32)
        begin = jnp.int32(0)
        for m in range(IMAGES):
            tally = counts[0, m]
            inner = row - begin
            hit = (inner == place) & (place < tally)
            label = (perm[m : m + 1, :] + m * PATCHES).astype(F32)
            found = found + jnp.where(hit, label, 0.0)
            mine = (row_line >= begin) & (row_line < begin + tally)
            owned = owned + jnp.where(mine, tally.astype(F32), 0.0)
            begin = begin + tally
        flat = jnp.sum(found, axis=1, keepdims=True).astype(jnp.int32)
        weight_out[...] = 1.0 / owned
        choice = lax.broadcasted_iota(jnp.int32, (ROWS, IMAGES * PATCHES), 1) == flat
        choice = jnp.where(choice, 1.0, 0.0).astype(BF16)
        t_rows = jnp.dot(choice, teacher[...].reshape(IMAGES * PATCHES, BOT), preferred_element_type=F32)
        ht[...] = unit_rows(t_rows)[0].astype(BF16)
        s_rows = jnp.dot(choice, student[...].reshape(IMAGES * PATCHES, BOT), preferred_element_type=F32)
        rows_out[...] = s_rows
        zs = unit_rows(s_rows)[0]
        hs_out[...] = zs.astype(BF16)
        turned = zs.T.reshape(NZ, 2, NB, ROWS)
        even = turned[:, 0].reshape(BOT // 2, ROWS)
        odd = turned[:, 1].reshape(BOT // 2, ROWS)
        first = core[0] == 0
        keep_out[...] = jnp.where(first, even, odd).astype(BF16)
        send_out[...] = jnp.where(first, odd, even).astype(BF16)

    sums = []
    for c in range(HALF // 256):
        at = slice(c * 256, (c + 1) * 256)
        e = jnp.exp(jnp.dot(ht[...], protos[:, at], preferred_element_type=F32) * 25.0)
        energy[:, at] = e
        sums += [e[:, :LANES], e[:, LANES:]]
    col_out[...] = jnp.broadcast_to(tile_sums(sums)[None], (NB, HALF // LANES, LANES))


def soft_body(hs, protos, out, acc):
    step = pl.program_id(0)
    part = jnp.zeros((ROWS, LANES), F32)
    for c in range(HALF // 256):
        at = slice(c * 256, (c + 1) * 256)
        e = jnp.exp(jnp.dot(hs[...], protos[:, at], preferred_element_type=F32) * 10.0)
        part = part + e[:, :LANES] + e[:, LANES:]

    @pl.when(step == 0)
    def _():
        acc[...] = part

    @pl.when(step == 1)
    def _():
        out[...] = to_line(acc[...] + part)


def row_work(cols, energy, acc):
    scale = 1.0 / jnp.sum(cols[...], axis=0)
    part = jnp.zeros((ROWS, LANES), F32)
    for j in range(HALF // LANES):
        part = part + energy[:, j * LANES : (j + 1) * LANES] * scale[j : j + 1, :]

    @pl.when(pl.program_id(0) == 0)
    def _():
        acc[...] = part

    return part


def row_body(cols, energy, out, acc):
    part = row_work(cols, energy, acc)

    @pl.when(pl.program_id(0) == 1)
    def _():
        out[...] = jnp.broadcast_to(to_line(acc[...] + part)[None], (NP, 1, ROWS))


def row_soft_body(cols, energy, soft, out, acc):
    part = row_work(cols, energy, acc)

    @pl.when(pl.program_id(0) == 1)
    def _():
        line = jnp.concatenate([to_line(acc[...] + part), soft[...]], axis=1)
        out[...] = jnp.broadcast_to(line[None], (NP, 1, 2 * ROWS))


def col_body(rows, energy, out, scale):
    @pl.when(pl.program_id(0) == 0)
    def _():
        scale[...] = to_column(1.0 / jnp.sum(rows[:, :, :ROWS], axis=0))

    s = scale[...]
    sums = [energy[:, j * LANES : (j + 1) * LANES] * s for j in range(HALF // LANES)]
    out[...] = jnp.broadcast_to(tile_sums(sums)[None], (NB, HALF // LANES, LANES))


def grad_body(rows, softs, cols, energy, hs, hk, hx, weight, protos, keep, send, back, row_scale, soft_scale):
    step = pl.program_id(0)

    @pl.when(step == 0)
    def _():
        row_scale[...] = to_column(1.0 / jnp.sum(rows[...], axis=0))
        soft_scale[...] = to_column(1.0 / jnp.sum(softs[:, :, ROWS:], axis=0))
        back[...] = jnp.zeros((ROWS, BOT), F32)

    col_scale = 1.0 / jnp.sum(cols[...], axis=0)
    rs = row_scale[...]
    ss = soft_scale[...]
    factor = weight[...] * (K * 10.0)
    total = back[...]
    for c in range(HALF // 256):
        at = slice(c * 256, (c + 1) * 256)
        block = protos[:, at]
        expo = jnp.exp(jnp.dot(hs[...], block, preferred_element_type=F32) * 10.0)
        parts = []
        for h in range(2):
            j = 2 * c + h
            lane = slice(j * LANES, (j + 1) * LANES)
            soft = expo[:, h * LANES : (h + 1) * LANES] * ss
            target = rs * energy[:, lane] * col_scale[j : j + 1, :]
            parts.append((factor * (soft - target)).astype(BF16))
        g = jnp.concatenate(parts, axis=1)
        keep[:, :, at] = jnp.dot(hk[...], g, preferred_element_type=F32).reshape(NZ, NB, 256)
        send[:, :, at] = jnp.dot(hx[...], g, preferred_element_type=F32).reshape(NZ, NB, 256)
        total = total + lax.dot_general(g, block, (((1,), (1,)), ((), ())), preferred_element_type=F32)
    back[...] = total


def whole(shape):
    return pl.BlockSpec(shape, lambda i: (0,) * len(shape))


ENERGY = pl.BlockSpec((ROWS, HALF), lambda i: (0, i))
PROTOS = pl.BlockSpec((BOT, HALF), lambda i: (0, i))
COL = pl.BlockSpec((NB, HALF // LANES, LANES), lambda i: (0, i, 0))
COL_SHAPE = jax.ShapeDtypeStruct((NB, COLS // LANES, LANES), F32)
SMEM = pl.BlockSpec(memory_space=pltpu.SMEM)
PARAMS = pltpu.CompilerParams(dimension_semantics=("arbitrary",))


def call(body, name, ins, outs, shapes, scratch):
    return pl.pallas_call(
        body, grid=(2,), in_specs=ins, out_specs=outs, out_shape=shapes,
        scratch_shapes=scratch, compiler_params=PARAMS, name=name,
    )


def shape(dims, dtype=F32):
    return jax.ShapeDtypeStruct(dims, dtype)


def exchange(sent, axis):
    return lax.all_to_all(sent, axis, 0, 0, tiled=True)


def on_device(teacher, student, perm, counts, protos):
    member = lax.axis_index("batch")
    core = (member % 2).astype(jnp.int32).reshape(1)
    energy, col_sent, rows, hs, hk, hx, weight = call(
        start_body, "start",
        [SMEM, SMEM, whole((IMAGES, PATCHES)), whole((IMAGES, PATCHES, BOT)), whole((IMAGES, PATCHES, BOT)), PROTOS],
        [ENERGY, COL, whole((ROWS, BOT)), whole((ROWS, BOT)), whole((BOT // 2, ROWS)), whole((BOT // 2, ROWS)), whole((ROWS, LANES))],
        [shape((ROWS, COLS)), COL_SHAPE, shape((ROWS, BOT)), shape((ROWS, BOT), BF16), shape((BOT // 2, ROWS), BF16),
         shape((BOT // 2, ROWS), BF16), shape((ROWS, LANES))],
        [pltpu.VMEM((ROWS, BOT), BF16)],
    )(counts, core, perm, teacher, student, protos)
    soft_line = call(
        soft_body, "soft", [whole((ROWS, BOT)), PROTOS], whole((1, ROWS)), shape((1, ROWS)), [pltpu.VMEM((ROWS, LANES), F32)]
    )(hs, protos)
    column = pltpu.VMEM((ROWS, LANES), F32)
    softs = None
    for sweep in range(SWEEPS):
        cols = exchange(col_sent, "batch")
        if sweep == 0:
            sent = call(
                row_soft_body, "rowsoft", [COL, ENERGY, whole((1, ROWS))], whole((NP, 1, 2 * ROWS)),
                shape((NP, 1, 2 * ROWS)), [column],
            )(cols, energy, soft_line)
        else:
            sent = call(row_body, "row", [COL, ENERGY], whole((NP, 1, ROWS)), shape((NP, 1, ROWS)), [column])(cols, energy)
        got = exchange(sent, "proto")
        if sweep == 0:
            softs = got
        if sweep < SWEEPS - 1:
            col_sent = call(col_body, "col", [whole(got.shape), ENERGY], COL, COL_SHAPE, [column])(got, energy)
    piece = pl.BlockSpec((NZ, NB, HALF), lambda i: (0, 0, i))
    keep, send, back = call(
        grad_body, "grad",
        [whole((NP, 1, ROWS)), whole((NP, 1, 2 * ROWS)), COL, ENERGY, whole((ROWS, BOT)), whole((BOT // 2, ROWS)),
         whole((BOT // 2, ROWS)), whole((ROWS, LANES)), PROTOS],
        [piece, piece, whole((ROWS, BOT))],
        [shape((NZ, NB, COLS)), shape((NZ, NB, COLS)), shape((ROWS, BOT))],
        [column, column],
    )(got, softs, cols, energy, hs, hk, hx, weight, protos)
    swap = [(b, b ^ 1) for b in range(NB)]
    share = ROWS // NP
    back_got = exchange(back.reshape(NP, share, BOT), "proto")
    pair = keep + lax.ppermute(send, "batch", swap)
    ring = [list(range(c, NB, 2)) for c in range(2)]
    proto_grad = lax.all_to_all(pair, "batch", 0, 0, axis_index_groups=ring, tiled=True).sum(axis=0)
    mine = lax.dynamic_slice_in_dim(rows, lax.axis_index("proto") * share, share, 0)
    unit, inverse = unit_rows(mine)
    back_sum = back_got.sum(axis=0)
    feature_grad = inverse * (back_sum - unit * jnp.sum(unit * back_sum, axis=1, keepdims=True))
    return (feature_grad, proto_grad)


def solution(mesh):
    in_specs = (
        P("batch", None, None),
        P("batch", None, None),
        P("batch", None),
        P("batch", None),
        P(None, "proto"),
    )
    out_specs = (P(("batch", "proto"), None), P("batch", "proto"))
    return jax.shard_map(
        on_device, mesh=mesh, in_specs=in_specs, out_specs=out_specs, check_vma=False
    )
```

```python
import jax
import jax.numpy as jnp
from jax import lax
from jax.experimental import pallas as pl
from jax.experimental.pallas import tpu as pltpu
from jax.sharding import PartitionSpec as P

K = 131072
SWEEPS = 3
ROWS = 384
BOT = 256
COLS = 2048
PATCHES = 256
IMAGES = 4
HALF = COLS // 2
LANES = 128
NB = 16
NP = 64
NZ = 8
SHARE = ROWS // NP
F32 = jnp.float32
BF16 = jnp.bfloat16


def unit_rows(values):
    inverse = lax.rsqrt(jnp.sum(values * values, axis=1, keepdims=True) + 1e-06)
    return values * inverse, inverse


def to_column(line):
    return jnp.broadcast_to(line, (LANES, ROWS)).T


def to_line(part):
    return jnp.sum(part.T, axis=0, keepdims=True)


def tile_sums(part):
    return jnp.concatenate([jnp.sum(p, axis=0, keepdims=True) for p in part], axis=0)


def start_body(counts, place_of, perm, teacher, student, protos, energy, col_out, rows_out, hs_out, keep_out, send_out, weight_out, ht):
    @pl.when(pl.program_id(0) == 0)
    def _():
        row = lax.broadcasted_iota(jnp.int32, (ROWS, PATCHES), 0)
        place = lax.broadcasted_iota(jnp.int32, (ROWS, PATCHES), 1)
        row_line = lax.broadcasted_iota(jnp.int32, (ROWS, LANES), 0)
        found = jnp.zeros((ROWS, PATCHES), F32)
        owned = jnp.zeros((ROWS, LANES), F32)
        begin = jnp.int32(0)
        for m in range(IMAGES):
            tally = counts[0, m]
            inner = row - begin
            hit = (inner == place) & (place < tally)
            label = (perm[m : m + 1, :] + m * PATCHES).astype(F32)
            found = found + jnp.where(hit, label, 0.0)
            mine = (row_line >= begin) & (row_line < begin + tally)
            owned = owned + jnp.where(mine, tally.astype(F32), 0.0)
            begin = begin + tally
        flat = jnp.sum(found, axis=1, keepdims=True).astype(jnp.int32)
        weight_out[...] = 1.0 / owned
        choice = lax.broadcasted_iota(jnp.int32, (ROWS, IMAGES * PATCHES), 1) == flat
        choice = jnp.where(choice, 1.0, 0.0).astype(BF16)
        t_rows = jnp.dot(choice, teacher[...].reshape(IMAGES * PATCHES, BOT), preferred_element_type=F32)
        ht[...] = unit_rows(t_rows)[0].astype(BF16)
        s_rows = jnp.dot(choice, student[...].reshape(IMAGES * PATCHES, BOT), preferred_element_type=F32)
        rows_out[...] = s_rows
        zs = unit_rows(s_rows)[0]
        hs_out[...] = zs.astype(BF16)
        turned = zs.T.reshape(NZ // 2, 2, 2, NB, ROWS)
        first = place_of[0] == 0
        same = place_of[1] == 0
        kept = []
        sent = []
        for z in range(2):
            low = jnp.where(same, turned[:, z], turned[:, 1 - z])
            even = low[:, 0].reshape(BOT // 4, ROWS)
            odd = low[:, 1].reshape(BOT // 4, ROWS)
            kept.append(jnp.where(first, even, odd))
            sent.append(jnp.where(first, odd, even))
        keep_out[...] = jnp.concatenate(kept, axis=0).astype(BF16)
        send_out[...] = jnp.concatenate(sent, axis=0).astype(BF16)

    sums = []
    for c in range(HALF // 256):
        at = slice(c * 256, (c + 1) * 256)
        e = jnp.exp(jnp.dot(ht[...], protos[:, at], preferred_element_type=F32) * 25.0)
        energy[:, at] = e
        sums += [e[:, :LANES], e[:, LANES:]]
    col_out[...] = jnp.broadcast_to(tile_sums(sums)[None], (NB, HALF // LANES, LANES))


def soft_body(hs, protos, out, acc):
    step = pl.program_id(0)
    part = jnp.zeros((ROWS, LANES), F32)
    for c in range(HALF // 256):
        at = slice(c * 256, (c + 1) * 256)
        e = jnp.exp(jnp.dot(hs[...], protos[:, at], preferred_element_type=F32) * 10.0)
        part = part + e[:, :LANES] + e[:, LANES:]

    @pl.when(step == 0)
    def _():
        acc[...] = part

    @pl.when(step == 1)
    def _():
        out[...] = to_line(acc[...] + part)


def row_work(cols, energy, acc):
    scale = 1.0 / jnp.sum(cols[...], axis=0)
    part = jnp.zeros((ROWS, LANES), F32)
    for j in range(HALF // LANES):
        part = part + energy[:, j * LANES : (j + 1) * LANES] * scale[j : j + 1, :]

    @pl.when(pl.program_id(0) == 0)
    def _():
        acc[...] = part

    return part


def row_body(cols, energy, out, acc):
    part = row_work(cols, energy, acc)

    @pl.when(pl.program_id(0) == 1)
    def _():
        out[...] = jnp.broadcast_to(to_line(acc[...] + part)[None], (NP, 1, ROWS))


def row_soft_body(cols, energy, soft, out, acc):
    part = row_work(cols, energy, acc)

    @pl.when(pl.program_id(0) == 1)
    def _():
        line = jnp.concatenate([to_line(acc[...] + part), soft[...]], axis=1)
        out[...] = jnp.broadcast_to(line[None], (NP, 1, 2 * ROWS))


def col_body(rows, energy, out, scale):
    @pl.when(pl.program_id(0) == 0)
    def _():
        scale[...] = to_column(1.0 / jnp.sum(rows[:, :, :ROWS], axis=0))

    s = scale[...]
    sums = [energy[:, j * LANES : (j + 1) * LANES] * s for j in range(HALF // LANES)]
    out[...] = jnp.broadcast_to(tile_sums(sums)[None], (NB, HALF // LANES, LANES))


def grad_body(rows, softs, cols, energy, hs, hk, hx, weight, protos, near, far, send, back_out, row_scale, soft_scale, back):
    step = pl.program_id(0)

    @pl.when(step == 0)
    def _():
        row_scale[...] = to_column(1.0 / jnp.sum(rows[...], axis=0))
        soft_scale[...] = to_column(1.0 / jnp.sum(softs[:, :, ROWS:], axis=0))
        back[...] = jnp.zeros((ROWS, BOT), F32)

    col_scale = 1.0 / jnp.sum(cols[...], axis=0)
    rs = row_scale[...]
    ss = soft_scale[...]
    factor = weight[...] * (K * 10.0)
    total = back[...]
    for c in range(HALF // 256):
        at = slice(c * 256, (c + 1) * 256)
        block = protos[:, at]
        expo = jnp.exp(jnp.dot(hs[...], block, preferred_element_type=F32) * 10.0)
        parts = []
        for h in range(2):
            j = 2 * c + h
            lane = slice(j * LANES, (j + 1) * LANES)
            soft = expo[:, h * LANES : (h + 1) * LANES] * ss
            target = rs * energy[:, lane] * col_scale[j : j + 1, :]
            parts.append((factor * (soft - target)).astype(BF16))
        g = jnp.concatenate(parts, axis=1)
        kept = jnp.dot(hk[...], g, preferred_element_type=F32).reshape(NZ, NB, 256)
        near[:, :, at] = kept[: NZ // 2]
        far[:, :, at] = kept[NZ // 2 :]
        send[:, :, at] = jnp.dot(hx[...], g, preferred_element_type=F32).reshape(NZ, NB, 256)
        total = total + lax.dot_general(g, block, (((1,), (1,)), ((), ())), preferred_element_type=F32)
    back[...] = total

    @pl.when(step == 1)
    def _():
        for p in range(NP):
            back_out[p] = back[p * SHARE : (p + 1) * SHARE, :]


def whole(shape):
    return pl.BlockSpec(shape, lambda i: (0,) * len(shape))


ENERGY = pl.BlockSpec((ROWS, HALF), lambda i: (0, i))
PROTOS = pl.BlockSpec((BOT, HALF), lambda i: (0, i))
COL = pl.BlockSpec((NB, HALF // LANES, LANES), lambda i: (0, i, 0))
COL_SHAPE = jax.ShapeDtypeStruct((NB, COLS // LANES, LANES), F32)
SMEM = pl.BlockSpec(memory_space=pltpu.SMEM)
PARAMS = pltpu.CompilerParams(dimension_semantics=("arbitrary",))


def call(body, ins, outs, shapes, scratch):
    return pl.pallas_call(
        body, grid=(2,), in_specs=ins, out_specs=outs, out_shape=shapes,
        scratch_shapes=scratch, compiler_params=PARAMS,
    )


def shape(dims, dtype=F32):
    return jax.ShapeDtypeStruct(dims, dtype)


def exchange(sent, axis):
    return lax.all_to_all(sent, axis, 0, 0, tiled=True)


def on_device(teacher, student, perm, counts, protos):
    member = lax.axis_index("batch")
    place_of = jnp.stack([member % 2, member // 2 % 2]).astype(jnp.int32)
    energy, col_sent, rows, hs, hk, hx, weight = call(
        start_body,
        [SMEM, SMEM, whole((IMAGES, PATCHES)), whole((IMAGES, PATCHES, BOT)), whole((IMAGES, PATCHES, BOT)), PROTOS],
        [ENERGY, COL, whole((ROWS, BOT)), whole((ROWS, BOT)), whole((BOT // 2, ROWS)), whole((BOT // 2, ROWS)), whole((ROWS, LANES))],
        [shape((ROWS, COLS)), COL_SHAPE, shape((ROWS, BOT)), shape((ROWS, BOT), BF16), shape((BOT // 2, ROWS), BF16),
         shape((BOT // 2, ROWS), BF16), shape((ROWS, LANES))],
        [pltpu.VMEM((ROWS, BOT), BF16)],
    )(counts, place_of, perm, teacher, student, protos)
    soft_line = call(
        soft_body, [whole((ROWS, BOT)), PROTOS], whole((1, ROWS)), shape((1, ROWS)), [pltpu.VMEM((ROWS, LANES), F32)]
    )(hs, protos)
    column = pltpu.VMEM((ROWS, LANES), F32)
    softs = None
    for sweep in range(SWEEPS):
        cols = exchange(col_sent, "batch")
        if sweep == 0:
            sent = call(
                row_soft_body, [COL, ENERGY, whole((1, ROWS))], whole((NP, 1, 2 * ROWS)),
                shape((NP, 1, 2 * ROWS)), [column],
            )(cols, energy, soft_line)
        else:
            sent = call(row_body, [COL, ENERGY], whole((NP, 1, ROWS)), shape((NP, 1, ROWS)), [column])(cols, energy)
        got = exchange(sent, "proto")
        if sweep == 0:
            softs = got
        if sweep < SWEEPS - 1:
            col_sent = call(col_body, [whole(got.shape), ENERGY], COL, COL_SHAPE, [column])(got, energy)
    piece = pl.BlockSpec((NZ, NB, HALF), lambda i: (0, 0, i))
    half_piece = pl.BlockSpec((NZ // 2, NB, HALF), lambda i: (0, 0, i))
    near, far, send, back = call(
        grad_body,
        [whole((NP, 1, ROWS)), whole((NP, 1, 2 * ROWS)), COL, ENERGY, whole((ROWS, BOT)), whole((BOT // 2, ROWS)),
         whole((BOT // 2, ROWS)), whole((ROWS, LANES)), PROTOS],
        [half_piece, half_piece, piece, whole((NP, SHARE, BOT))],
        [shape((NZ // 2, NB, COLS)), shape((NZ // 2, NB, COLS)), shape((NZ, NB, COLS)), shape((NP, SHARE, BOT))],
        [column, column, pltpu.VMEM((ROWS, BOT), F32)],
    )(got, softs, cols, energy, hs, hk, hx, weight, protos)
    swap = [(b, b ^ 1) for b in range(NB)]
    beside = [(b, b ^ 2) for b in range(NB)]
    swapped = lax.ppermute(send, "batch", swap)
    back_got = exchange(back, "proto")
    onward = far + swapped[NZ // 2 :]
    moved = lax.ppermute(onward, "batch", beside)
    four = near + swapped[: NZ // 2] + moved
    groups = [[c + 4 * z for z in range(4)] for c in range(4)]
    arrived = lax.all_to_all(four, "batch", 0, 0, axis_index_groups=groups, tiled=True)
    proto_grad = arrived.sum(axis=0)
    mine = lax.dynamic_slice_in_dim(rows, lax.axis_index("proto") * SHARE, SHARE, 0)
    unit, inverse = unit_rows(mine)
    back_sum = back_got.sum(axis=0)
    feature_grad = inverse * (back_sum - unit * jnp.sum(unit * back_sum, axis=1, keepdims=True))
    return (feature_grad, proto_grad)


def solution(mesh):
    in_specs = (
        P("batch", None, None),
        P("batch", None, None),
        P("batch", None),
        P("batch", None),
        P(None, "proto"),
    )
    out_specs = (P(("batch", "proto"), None), P("batch", "proto"))
    return jax.shard_map(
        on_device, mesh=mesh, in_specs=in_specs, out_specs=out_specs, check_vma=False
    )
```
